128 devices in a mesh: section: 8 (over z, x_hi), expert: 16 (over x_lo, y, core).
Axes of the slice: x: 4 (x_hi: 2, x_lo: 2; x = x_hi * 2 + x_lo), y: 4, z: 4, core: 2. Of those that a mesh axis runs over, the one named last changes fastest.
Arguments:
- layer_inputs: bfloat16 [8, 2, 1024, 2560], P('section', None, 'expert'), may hold values from -6 to 6
- norm_gain: float32 [8, 2560], P('section'), may hold values from 0.1 to 1.9
- routing: int32 [8, 2, 1024, 6], P('section', None, 'expert'), may hold values from 0 to 15, all different within a row; in each aligned block of 64 rows (0 to 63, 64 to 127, ..., all dimensions but the last counted through in order) at most 40 rows name the same one
- route_weight: float32 [8, 2, 1024, 6], P('section', None, 'expert'), may hold values from 0.05 to 0.6
- w_gate: bfloat16 [8, 16, 2560, 768], P('section', 'expert'), may hold values from -0.125 to 0.125
- w_up: bfloat16 [8, 16, 2560, 768], P('section', 'expert'), may hold values from -0.125 to 0.125
- w_down: bfloat16 [8, 16, 768, 2560], P('section', 'expert'), may hold values from -0.21875 to 0.21875
- top_grad: bfloat16 [2, 1024, 2560], P(None, 'expert'), may hold values from -6 to 6
Outputs:
- layer_grads: bfloat16 [8, 2, 1024, 2560], P('section', None, 'expert')
The draws below stay inside these ranges and needn't reach their ends.
Inputs may be any that keep to these rules, and one draw needn't show every extreme that they name: `routing`: in each aligned block of 64 rows (one device's tokens of one micro-batch in one layer) no expert is named by more than 40 rows, a bound that some block reaches.
All inputs are finite; a program needn't handle non-finite values.
Results may differ from the reference program's by a relative error of at most 0.025.
Values may be sent and summed in bfloat16 or wider, within the bound.
A program may use at most 128 MiB of HBM per device.

```python
import math
import jax
import jax.numpy as jnp
import numpy as np
from jax import lax

D = 2560
H = 768
TOP = 6
M = 2
TOK_MB = 64
EXPERTS = 16
TOKENS = 1024
CAP = 40
LAYERS = 8
N_EXPERT = 16


def block_scale(rng, dims, shards, least, largest):
    factor_of, own = 1.0, jax.random.fold_in(rng, 6)
    for dim, blocks in shards:
        heights = jnp.exp(jax.random.uniform(jax.random.fold_in(own, dim), (blocks,), jnp.float32, least / len(shards), largest / len(shards)))
        factor_of = factor_of * jnp.repeat(heights, dims[dim] // blocks).reshape([-1 if axis == dim else 1 for axis in range(len(dims))])
    return factor_of


def assign_block(rng, own, number, rows, count, top, reach, skew):
    ranking = jax.random.permutation(rng, count)
    heavy_load, common = portions_of(count, rows * top, reach, skew, True), portions_of(count, rows * top, reach, skew, False)
    places = jnp.arange(count)

    def named(lengths, turn):
        used = int((lengths > 0).sum())
        fixed = max(1, used // 4)
        passed = fixed + (places - fixed + turn * (used - fixed)) % max(1, count - fixed)
        return jnp.zeros((count,), jnp.int32).at[ranking[jnp.where(places < fixed, places, passed)]].set(jnp.asarray(lengths, jnp.int32))

    lengths = jnp.where(number % 4 == 0, named(heavy_load, number // 4), named(common, number - number // 4 - 1))
    mixed = jax.random.permutation(jax.random.fold_in(own, 3), count)
    source_of, sink = mixed[0:count // 2 * 2:2], mixed[1:count // 2 * 2:2]
    room = jnp.minimum(lengths[source_of] - 1, reach - lengths[sink]) // 2
    room = jnp.where((source_of == ranking[0]) | (sink == ranking[0]) | (lengths[sink] == 0), 0, jnp.maximum(room, 0))
    passed = jax.random.randint(jax.random.fold_in(own, 4), (count // 2,), 0, 1 << 20) % (room + 1)
    lengths = lengths.at[source_of].add(-passed).at[sink].add(passed)
    labels = jnp.searchsorted(jnp.cumsum(lengths), jnp.arange(rows * top), side="right").astype(jnp.int32)
    listing = labels.reshape(top, rows).T
    listing = listing[jax.random.permutation(jax.random.fold_in(own, 1), rows)]
    turn = jax.random.randint(jax.random.fold_in(own, 2), (rows, 1), 0, top)
    return jnp.take_along_axis(listing, (jnp.arange(top)[None, :] + turn) % top, axis=1)


def portions_of(amount, total, limit, slope, full):
    loads = [(1 << 20) // math.isqrt(rank ** slope) + 1 for rank in range(1, amount + 1)]
    largest = limit if full else min(limit, max(-(-total // amount), total * loads[0] // sum(loads)))
    least = 1 if total - largest >= amount - 1 else 0
    counts, spare = [largest] + [least] * (amount - 1), total - largest - least * (amount - 1)
    while spare > 0:
        movable = [i for i in range(1, amount) if counts[i] < largest] or [i for i in range(1, amount) if counts[i] < limit]
        whole, left = sum([loads[i] for i in movable]), spare
        for i in movable:
            addition = min(limit - counts[i], max(1, left * loads[i] // whole), spare)
            counts[i] = counts[i] + addition
            spare = spare - addition
    return np.array(counts)


def normal_values(own_key, extent, scale, limit, cuts=(), held_as=jnp.bfloat16):
    array = scale * jax.random.normal(own_key, extent, jnp.float32)
    if cuts:
        array = array * block_scale(own_key, extent, cuts, -0.22, 0.18)
    return jnp.clip(array, -limit, limit).astype(held_as)


def setup_inputs(seed: int = 0) -> dict:
    seeds = jax.random.split(jax.random.key(seed), 9)
    layer_inputs = normal_values(seeds[0], (LAYERS, M, TOKENS, D), 1.0, 6.0, ((0, 8), (2, 16)))
    norm_gain = jnp.clip(1.0 + 0.18 * jax.random.normal(seeds[1], (LAYERS, D), jnp.float32), 0.1, 1.9)
    routing_keys = jax.random.split(jax.random.fold_in(seeds[2], 1), LAYERS * M * TOKENS // TOK_MB)
    routing_turns = jax.random.permutation(jax.random.fold_in(seeds[2], 3), LAYERS * M * TOKENS // TOK_MB)
    routing = jax.vmap(lambda own, number: assign_block(jax.random.fold_in(seeds[2], 2), own, number, TOK_MB, EXPERTS, TOP, CAP, 2))(routing_keys, routing_turns).reshape((LAYERS, M, TOKENS, TOP))
    route_weight = jnp.clip(jnp.exp(math.log(0.6) - 2.4849067 * jax.random.uniform(seeds[3], (LAYERS, M, TOKENS, TOP), jnp.float32) ** block_scale(seeds[3], (LAYERS, M, TOKENS, TOP), ((0, 8), (2, 16)), -0.2, 0.2)), 0.05, 0.6)
    w_gate = normal_values(seeds[4], (LAYERS, EXPERTS, D, H), D ** -0.5, 0.125, ((0, 8), (1, 16)))
    w_up = normal_values(seeds[5], (LAYERS, EXPERTS, D, H), D ** -0.5, 0.125, ((0, 8), (1, 16)))
    w_down = normal_values(seeds[6], (LAYERS, EXPERTS, H, D), H ** -0.5, 0.21875, ((0, 8), (1, 16)))
    top_grad = normal_values(seeds[7], (M, TOKENS, D), 1.0, 6.0, ((1, 16),))
    return {"layer_inputs": layer_inputs, "norm_gain": norm_gain, "routing": routing, "route_weight": route_weight, "w_gate": w_gate, "w_up": w_up, "w_down": w_down, "top_grad": top_grad}


EPSILON = 1e-06

def norm_parts(inputs, gain_row):
    values = inputs.astype(jnp.float32)
    scale = lax.rsqrt(lax.optimization_barrier(jnp.mean(values * values, axis=-1, keepdims=True)) + EPSILON)
    normed = (values * scale * gain_row).astype(jnp.bfloat16)
    return (values, scale, normed)

def norm_back(values, scale, gain_row, upstream):
    scaled = gain_row * upstream
    return scale * scaled - values * scale ** 3 * lax.optimization_barrier(jnp.mean(values * scaled, axis=-1, keepdims=True))

def expert_back(x_rows, g_rows, gate_mat, up_mat, down_mat):
    pre_gate = jnp.dot(x_rows, gate_mat, preferred_element_type=jnp.float32)
    pre_up = jnp.dot(x_rows, up_mat, preferred_element_type=jnp.float32)
    hidden_grad = lax.dot_general(g_rows, down_mat, (((1,), (1,)), ((), ())), preferred_element_type=jnp.float32)
    sigma = jax.nn.sigmoid(pre_gate)
    grad_gate = (hidden_grad * pre_up * sigma * (1.0 + pre_gate * (1.0 - sigma))).astype(jnp.bfloat16)
    grad_up = (hidden_grad * pre_gate * sigma).astype(jnp.bfloat16)
    result = lax.dot_general(grad_gate, gate_mat, (((1,), (1,)), ((), ())), preferred_element_type=jnp.float32)
    result = result + lax.dot_general(grad_up, up_mat, (((1,), (1,)), ((), ())), preferred_element_type=jnp.float32)
    return result.astype(jnp.bfloat16)

def layer_back(inputs, gain_row, chosen, weights, gate_all, up_all, down_all, grad_in):
    values, scale, normed = norm_parts(inputs, gain_row)
    token_count = inputs.shape[0]
    flat = chosen.reshape(-1)
    row_count = flat.shape[0]
    width = CAP * N_EXPERT
    x_pad = jnp.concatenate([normed, jnp.zeros((1, D), normed.dtype)], 0)
    g_pad = jnp.concatenate([grad_in, jnp.zeros((1, D), grad_in.dtype)], 0)
    w_pad = jnp.concatenate([weights.reshape(-1), jnp.zeros((1,), jnp.float32)], 0)

    def single(expert_id):
        rows = jnp.nonzero(flat == expert_id, size=width, fill_value=row_count)[0].astype(jnp.int32)
        owners = (rows // TOP).astype(jnp.int32)
        result = expert_back(x_pad[owners], g_pad[owners], gate_all[expert_id], up_all[expert_id], down_all[expert_id])
        return (owners, result.astype(jnp.float32) * w_pad[rows][:, None])
    owners, parts = lax.map(single, jnp.arange(EXPERTS, dtype=jnp.int32))
    summed = jnp.zeros((token_count + 1, D), jnp.float32).at[owners.reshape(-1)].add(parts.reshape(-1, D))
    upstream = summed[:token_count]
    return (grad_in.astype(jnp.float32) + norm_back(values, scale, gain_row, upstream)).astype(jnp.bfloat16)

def reference(layer_inputs, norm_gain, routing, route_weight, w_gate, w_up, w_down, top_grad):
    sections = layer_inputs.shape[0]
    results = [None] * sections
    current = [top_grad[index] for index in range(M)]
    for depth_now in range(sections - 1, -1, -1):
        holder = (depth_now + sections // 2) % sections
        for index in range(M):
            current[index] = layer_back(layer_inputs[holder, index], norm_gain[holder], routing[holder, index], route_weight[holder, index], w_gate[holder], w_up[holder], w_down[holder], current[index])
        results[holder] = jnp.stack(current)
    return jnp.stack(results)
```

```python
import jax
import jax.numpy as jnp
from jax import lax
from jax.experimental import pallas as pl
from jax.experimental.pallas import tpu as pltpu
from jax.sharding import PartitionSpec as P

EPSILON = 1e-06
ROWS = 16
NT = (((1,), (1,)), ((), ()))
NN = (((1,), (0,)), ((), ()))
F32 = jnp.float32
BF16 = jnp.bfloat16
MESH = pl.DeviceIdType.MESH
PEERS = 8
COLS = 512


def opposite(j):
    dx, dy = divmod(j, 4)
    return dx * 4 + (4 - dy) % 4


def wait_bytes(ref, sem):
    pltpu.make_async_copy(ref, ref, sem).wait()


def window_kernel(
    x_ref, gain_ref, routing_ref, weight_ref, gate_hbm, up_hbm, down_hbm, top_hbm, out_ref,
    gate, up, down, factors, xb, cb, ag, rs_out, rs_in, hid,
    local_sem, wsend, wrecv, top_sem, xsend, xrecv, csend, crecv,
    gsend, grecv, rsend, rrecv, lsend, lrecv,
):
    chunks = x_ref.shape[0]
    width = x_ref.shape[2]
    section = lax.axis_index("section")
    me = lax.axis_index("expert")
    sections = lax.axis_size("section")
    depth = lax.rem(section + sections // 2, sections)
    below = lax.rem(section + sections - 1, sections)
    above = lax.rem(section + 1, sections)
    core = lax.rem(me, 2)
    row = lax.rem(me // 2, 4)
    side = me // 8
    partner = me + 1 - 2 * core
    is_top = depth == sections - 1

    def peer(j):
        dx, dy = divmod(j, 4)
        return lax.rem(side + dx, 2) * 8 + lax.rem(row + dy, 4) * 2 + core

    pairs = [(gate_hbm, gate), (up_hbm, up), (down_hbm, down)]
    for n, (src, dst) in enumerate(pairs):
        pltpu.make_async_copy(src, dst.at[0], local_sem.at[n]).start()

    barrier = pltpu.get_barrier_semaphore()
    for j in range(1, PEERS):
        pl.semaphore_signal(barrier, inc=1, device_id=(section, peer(j)), device_id_type=MESH)
    pl.semaphore_signal(barrier, inc=1, device_id=(section, partner), device_id_type=MESH)
    pl.semaphore_signal(barrier, inc=1, device_id=(below, me), device_id_type=MESH)
    pl.semaphore_signal(barrier, inc=1, device_id=(above, me), device_id_type=MESH)

    @pl.when(is_top)
    def _():
        for c in range(chunks):
            pltpu.make_async_copy(top_hbm.at[c], ag.at[c, 0], top_sem.at[c]).start()

    gain = gain_ref[...]

    def local_part(c, _):
        x = x_ref[c].astype(F32)
        scale = lax.rsqrt(jnp.mean(x * x, axis=-1, keepdims=True) + EPSILON)
        xb[c, 0] = (x * scale * gain).astype(BF16)
        chosen = routing_ref[c]
        weights = weight_ref[c]
        lanes = lax.broadcasted_iota(jnp.int32, (ROWS, 128), 1)
        coef = jnp.zeros((ROWS, 128), F32)
        for k in range(chosen.shape[1]):
            coef = coef + jnp.where(lanes == chosen[:, k : k + 1], weights[:, k : k + 1], 0.0)
        cb[c, 0] = coef
        return 0

    lax.fori_loop(0, chunks, local_part, 0)
    pl.semaphore_wait(barrier, PEERS + 2)

    weight_copies = []
    for n, (src, dst) in enumerate(pairs):
        copy = pltpu.make_async_remote_copy(
            src_ref=src, dst_ref=dst.at[1], send_sem=wsend.at[n], recv_sem=wrecv.at[n],
            device_id=(section, partner), device_id_type=MESH,
        )
        copy.start()
        weight_copies.append(copy)

    def spread(buf, c, send, recv):
        for j in range(1, PEERS):
            pltpu.make_async_remote_copy(
                src_ref=buf.at[c, 0], dst_ref=buf.at[c, opposite(j)],
                send_sem=send.at[c], recv_sem=recv.at[c],
                device_id=(section, peer(j)), device_id_type=MESH,
            ).start()

    def send_inputs(c, _):
        spread(cb, c, csend, crecv)
        spread(xb, c, xsend, xrecv)

        @pl.when(is_top)
        def _():
            wait_bytes(ag.at[c, 0], top_sem.at[c])
            spread(ag, c, gsend, grecv)

        return 0

    lax.fori_loop(0, chunks, send_inputs, 0)

    for n, (src, dst) in enumerate(pairs):
        pltpu.make_async_copy(src, dst.at[0], local_sem.at[n]).wait()
        weight_copies[n].wait_recv()

    others = pl.ds(1, PEERS - 1)

    def prepare(c):
        wait_bytes(cb.at[c, others], crecv.at[c])
        wait_bytes(xb.at[c, others], xrecv.at[c])
        x = xb[c].reshape(PEERS * ROWS, width)
        coef = cb[c].reshape(PEERS * ROWS, 128)
        lanes = lax.broadcasted_iota(jnp.int32, coef.shape, 1)
        for n, owner in enumerate((me, partner)):
            part = jnp.sum(jnp.where(lanes == owner, coef, 0.0), axis=-1, keepdims=True)
            pre_gate = lax.dot_general(x, gate[n], NN, preferred_element_type=F32)
            pre_up = lax.dot_general(x, up[n], NN, preferred_element_type=F32)
            q = jax.nn.sigmoid(pre_gate)
            factors[c, n, 0] = (part * pre_up * q * (1.0 + pre_gate * (1.0 - q))).astype(BF16)
            factors[c, n, 1] = (part * pre_gate * q).astype(BF16)

    def start_gather(c):
        wait_bytes(ag.at[c, 0], lrecv.at[c])
        spread(ag, c, gsend, grecv)

    def compute(c):
        wait_bytes(ag.at[c, others], grecv.at[c])
        g = ag[c].reshape(PEERS * ROWS, width)
        for n in range(2):
            hidden = lax.dot_general(g, down[n], NT, preferred_element_type=F32)
            hid[n, 0] = (hidden * factors[c, n, 0].astype(F32)).astype(BF16)
            hid[n, 1] = (hidden * factors[c, n, 1].astype(F32)).astype(BF16)
        for col in range(0, width, COLS):
            total = jnp.zeros((PEERS * ROWS, COLS), F32)
            for n in range(2):
                for t, mat in enumerate((gate, up)):
                    total = total + lax.dot_general(
                        hid[n, t], mat[n, col : col + COLS, :], NT, preferred_element_type=F32
                    )
            rs_out[c, :, :, col : col + COLS] = total.astype(BF16).reshape(PEERS, ROWS, COLS)
        for j in range(1, PEERS):
            pltpu.make_async_remote_copy(
                src_ref=rs_out.at[c, j], dst_ref=rs_in.at[c, opposite(j)],
                send_sem=rsend.at[c], recv_sem=rrecv.at[c],
                device_id=(section, peer(j)), device_id_type=MESH,
            ).start()

    def relay(c):
        return pltpu.make_async_remote_copy(
            src_ref=out_ref.at[c], dst_ref=ag.at[c, 0], send_sem=lsend.at[c], recv_sem=lrecv.at[c],
            device_id=(below, me), device_id_type=MESH,
        )

    def finish(c):
        x = x_ref[c].astype(F32)
        scale = lax.rsqrt(jnp.mean(x * x, axis=-1, keepdims=True) + EPSILON)
        wait_bytes(rs_in.at[c, others], rrecv.at[c])
        dy = rs_out[c, 0].astype(F32)
        for j in range(1, PEERS):
            dy = dy + rs_in[c, j].astype(F32)
        scaled = gain * dy
        change = scale * scaled - x * scale**3 * jnp.mean(x * scaled, axis=-1, keepdims=True)
        out_ref[c] = (ag[c, 0].astype(F32) + change).astype(BF16)

        @pl.when(depth > 0)
        def _():
            relay(c).start()

    @pl.when(jnp.logical_not(is_top))
    def _():
        def body(c, _):
            prepare(c)
            return 0

        lax.fori_loop(0, chunks, body, 0)
        start_gather(0)

    def main(c, _):
        @pl.when(is_top)
        def _():
            prepare(c)

        compute(c)

        @pl.when(jnp.logical_and(jnp.logical_not(is_top), c + 1 < chunks))
        def _():
            start_gather(c + 1)

        finish(c)
        return 0

    lax.fori_loop(0, chunks, main, 0)

    def drain(c, _):
        wait_bytes(cb.at[c, others], csend.at[c])
        wait_bytes(xb.at[c, others], xsend.at[c])
        wait_bytes(ag.at[c, others], gsend.at[c])
        wait_bytes(rs_in.at[c, others], rsend.at[c])

        @pl.when(depth > 0)
        def _():
            wait_bytes(out_ref.at[c], lsend.at[c])

        return 0

    lax.fori_loop(0, chunks, drain, 0)
    for copy in weight_copies:
        copy.wait_send()


def per_device(layer_inputs, norm_gain, routing, route_weight, w_gate, w_up, w_down, top_grad):
    _, micro_count, token_count, width = layer_inputs.shape
    top_count = routing.shape[3]
    hidden = w_gate.shape[3]
    chunks = micro_count * token_count // ROWS
    vmem = pl.BlockSpec(memory_space=pltpu.VMEM)
    anyspace = pl.BlockSpec(memory_space=pl.ANY)
    dma = pltpu.SemaphoreType.DMA
    block = (chunks, PEERS, ROWS, width)
    out = pl.pallas_call(
        window_kernel,
        out_shape=jax.ShapeDtypeStruct((chunks, ROWS, width), BF16),
        in_specs=[vmem] * 4 + [anyspace] * 4,
        out_specs=vmem,
        scratch_shapes=[
            pltpu.VMEM((2, width, hidden), BF16),
            pltpu.VMEM((2, width, hidden), BF16),
            pltpu.VMEM((2, hidden, width), BF16),
            pltpu.VMEM((chunks, 2, 2, PEERS * ROWS, hidden), BF16),
            pltpu.VMEM(block, BF16),
            pltpu.VMEM((chunks, PEERS, ROWS, 128), F32),
            pltpu.VMEM(block, BF16),
            pltpu.VMEM(block, BF16),
            pltpu.VMEM(block, BF16),
            pltpu.VMEM((2, 2, PEERS * ROWS, hidden), BF16),
        ]
        + [dma((3,))] * 3
        + [dma((chunks,))] * 11,
        compiler_params=pltpu.CompilerParams(
            collective_id=0, has_side_effects=True, vmem_limit_bytes=67043328
        ),
    )(
        layer_inputs.reshape(chunks, ROWS, width),
        norm_gain,
        routing.reshape(chunks, ROWS, top_count),
        route_weight.reshape(chunks, ROWS, top_count),
        w_gate[0, 0],
        w_up[0, 0],
        w_down[0, 0],
        top_grad.reshape(chunks, ROWS, width),
    )
    return out.reshape(layer_inputs.shape)


def solution(mesh):
    placed = (
        P("section", None, "expert", None),
        P("section", None),
        P("section", None, "expert", None),
        P("section", None, "expert", None),
        P("section", "expert", None, None),
        P("section", "expert", None, None),
        P("section", "expert", None, None),
        P(None, "expert", None),
    )
    return jax.shard_map(
        per_device,
        mesh=mesh,
        in_specs=placed,
        out_specs=P("section", None, "expert", None),
        check_vma=False,
    )
```
